32 devices in a mesh: scene: 8 (over z, x), head: 4 (over y, core).
Axes of the slice: x: 2, y: 2, z: 4, core: 2. Of those that a mesh axis runs over, the one named last changes fastest.
Arguments:
- layer_in: bfloat16 [16384, 1024], P(('scene', 'head')), may hold values from -6 to 6
- scene_len: int32 [16], replicated, may hold values from 0 to 2048, as said below
- scene_group: int32 [16], replicated, may hold values from 0 to 7, as said below
- scene_off: int32 [16], replicated, may hold values from 0 to 2048, as said below
- w_qkv: bfloat16 [1024, 3072], replicated, may hold values from -0.1875 to 0.1875
- bias_q: bfloat16 [1024], replicated, may hold values from -3 to 3
- bias_v: bfloat16 [1024], replicated, may hold values from -3 to 3
- w_out: bfloat16 [1024, 1024], replicated, may hold values from -4 to 4
- bias_out: bfloat16 [1024], replicated, may hold values from -3 to 3
- w_up: bfloat16 [1024, 4096], replicated, may hold values from -0.1875 to 0.1875
- bias_up: bfloat16 [4096], replicated, may hold values from -3 to 3
- w_down: bfloat16 [4096, 1024], replicated, may hold values from -0.09375 to 0.09375
- bias_down: bfloat16 [1024], replicated, may hold values from -3 to 3
- gain_one: bfloat16 [1024], replicated, may hold values from 0.099609375 to 1.8984375
- shift_one: bfloat16 [1024], replicated, may hold values from -3 to 3
- gain_two: bfloat16 [1024], replicated, may hold values from 0.099609375 to 1.8984375
- shift_two: bfloat16 [1024], replicated, may hold values from -3 to 3
- grad_out: bfloat16 [16384, 1024], P(('scene', 'head')), may hold values from -6 to 6
Outputs:
- layer_out: bfloat16 [16384, 1024], P(('scene', 'head'))
- grad_in: bfloat16 [16384, 1024], P(('scene', 'head'))
- grad_w_qkv: float32 [1024, 3072], P(None, ('scene', 'head'))
- grad_bias_q: float32 [1024], P(('scene', 'head'))
- grad_bias_v: float32 [1024], P(('scene', 'head'))
- grad_w_out: float32 [1024, 1024], P(None, ('scene', 'head'))
- grad_bias_out: float32 [1024], P(('scene', 'head'))
- grad_w_up: float32 [1024, 4096], P(None, ('scene', 'head'))
- grad_bias_up: float32 [4096], P(('scene', 'head'))
- grad_w_down: float32 [4096, 1024], P(None, ('scene', 'head'))
- grad_bias_down: float32 [1024], P(('scene', 'head'))
- grad_gain_one: float32 [1024], P(('scene', 'head'))
- grad_shift_one: float32 [1024], P(('scene', 'head'))
- grad_gain_two: float32 [1024], P(('scene', 'head'))
- grad_shift_two: float32 [1024], P(('scene', 'head'))
The draws below stay inside these ranges and needn't reach their ends.
Inputs may be any that keep to these rules, and one draw needn't show every extreme that they name: `scene_len`: scene slots j and j + 8 lie in the same group; a nonempty scene has 1024 tokens or more; slot 0 fills its whole group in every draw. `scene_group`: the first 8 entries name every group once; the last 8 repeat them. `scene_off`: slot j starts at place 0 of its group and slot j + 8 right after it, so the scenes of a group are packed from its first place.
All inputs are finite; a program needn't handle non-finite values.
Results may differ from the reference program's by a relative error of at most 0.012.
Values may be sent and summed in bfloat16 or wider, within the bound.
No kernel may reach another device: no remote copies, remote signals or barrier semaphores. Data moves between devices by JAX's collectives and lax.ppermute only.
A program may use at most 192 MiB of HBM per device.

```python
import jax
import jax.numpy as jnp
from jax import lax

D = 1024
HEADS = 16
HEAD_DIM = 64
FF = 4096
CAPACITY = 2048
SCENE_MIN = 1024
SCENES = 16
TOKENS = 16384
N_SCENE = 8


def scene_layout(key):
    base = jax.random.fold_in(key, 29)
    first_key, second_key, order_key = jax.random.split(base, 3)
    first = jax.random.randint(first_key, (N_SCENE,), SCENE_MIN, CAPACITY + 1)
    first = jnp.where(jnp.arange(N_SCENE) == 0, CAPACITY, first)
    room = CAPACITY - first
    second = jax.random.randint(second_key, (N_SCENE,), SCENE_MIN, jnp.maximum(room, SCENE_MIN) + 1)
    second = jnp.where(room >= SCENE_MIN, second, 0)
    order = jax.random.permutation(order_key, N_SCENE)
    lengths = jnp.concatenate([first, second]).astype(jnp.int32)
    owners = jnp.concatenate([order, order]).astype(jnp.int32)
    offsets = jnp.concatenate([jnp.zeros((N_SCENE,), jnp.int32), first.astype(jnp.int32)]).astype(jnp.int32)
    return (lengths, owners, offsets)


def draw_scene_len(key, part):
    return scene_layout(key)[0]


def draw_scene_group(key, part):
    return scene_layout(key)[1]


def draw_scene_off(key, part):
    return scene_layout(key)[2]


def raised(entries, rng, source, target, shards_of, factor):
    owner, partner = [(jnp.arange(entries.shape[position]) // (entries.shape[position] // shards_of)).reshape([-1 if axis == position else 1 for axis in range(entries.ndim)]) for position in (source, target)]
    chosen = jax.random.permutation(rng, shards_of)[partner]
    strong = (owner == chosen) | (owner == (partner + shards_of // 2) % shards_of)
    return jnp.where(strong, factor * entries, entries)


def steps_of(own_key, dims, cuts, smallest, top_value):
    factor_of, own = 1.0, jax.random.fold_in(own_key, 6)
    for position, shards_of in cuts:
        heights = jnp.exp(jax.random.uniform(jax.random.fold_in(own, position), (shards_of,), jnp.float32, smallest / len(cuts), top_value / len(cuts)))
        factor_of = factor_of * jnp.repeat(heights, dims[position] // shards_of).reshape([-1 if axis == position else 1 for axis in range(len(dims))])
    return factor_of


def normal_values(key, dims, scale, reach, cuts=(), kind=jnp.bfloat16):
    level = steps_of(key, dims, cuts, -0.22, 0.18) if cuts else 1.0
    entries = jax.random.normal(key, dims, jnp.float32) * scale * level
    return jnp.minimum(jnp.maximum(entries, -reach), reach).astype(kind)


def noise_with(rng, dims, width, limit, cuts, heavy, kind=jnp.bfloat16):
    array = width * jax.random.normal(rng, dims, jnp.float32)
    if cuts:
        array = array * steps_of(rng, dims, cuts, -0.22, 0.18)
    return jnp.clip(raised(array, jax.random.fold_in(rng, 3), *heavy), -limit, limit).astype(kind)


def setup_inputs(seed: int = 0) -> dict:
    key_list = jax.random.split(jax.random.key(seed), 19)
    layer_in = normal_values(key_list[0], (TOKENS, D), 1.0, 6.0, ((0, 32),))
    scene_len = draw_scene_len(jax.random.fold_in(key_list[18], 71), 0)
    scene_group = draw_scene_group(jax.random.fold_in(key_list[18], 71), 0)
    scene_off = draw_scene_off(jax.random.fold_in(key_list[18], 71), 0)
    w_qkv = normal_values(key_list[4], (D, 3 * D), D ** -0.5, 0.1875)
    bias_q = normal_values(key_list[5], (D,), 0.5, 3.0)
    bias_v = normal_values(key_list[6], (D,), 0.5, 3.0)
    w_out = normal_values(key_list[7], (D, D), (max(1, D * 4 // CAPACITY)) ** -0.5, 4.0)
    bias_out = normal_values(key_list[8], (D,), 0.5, 3.0)
    w_up = normal_values(key_list[9], (D, FF), D ** -0.5, 0.1875)
    bias_up = normal_values(key_list[10], (FF,), 0.5, 3.0)
    w_down = normal_values(key_list[11], (FF, D), FF ** -0.5, 0.09375)
    bias_down = normal_values(key_list[12], (D,), 0.5, 3.0)
    gain_one = jnp.clip(1.0 + 0.18 * jax.random.normal(key_list[13], (D,), jnp.float32), 0.099609375, 1.8984375).astype(jnp.bfloat16)
    shift_one = normal_values(key_list[14], (D,), 0.5, 3.0)
    gain_two = jnp.clip(1.0 + 0.18 * jax.random.normal(key_list[15], (D,), jnp.float32), 0.099609375, 1.8984375).astype(jnp.bfloat16)
    shift_two = normal_values(key_list[16], (D,), 0.5, 3.0)
    grad_out = noise_with(key_list[17], (TOKENS, D), 1.0, 6.0, ((0, 32),), (0, 1, 32, 2.75))
    return dict(layer_in=layer_in, scene_len=scene_len, scene_group=scene_group, scene_off=scene_off, w_qkv=w_qkv, bias_q=bias_q, bias_v=bias_v, w_out=w_out, bias_out=bias_out, w_up=w_up, bias_up=bias_up, w_down=w_down, bias_down=bias_down, gain_one=gain_one, shift_one=shift_one, gain_two=gain_two, shift_two=shift_two, grad_out=grad_out)


@jax.custom_vjp
def low(v):
    return lax.optimization_barrier(v.astype(jnp.bfloat16)).astype(jnp.float32)

@jax.custom_vjp
def low_back(v):
    return v

def low_keep(v):
    return (low(v), None)

def low_pass(kept, grad):
    return (grad,)

def back_keep(v):
    return (v, None)

def back_low(kept, grad):
    return (low(grad),)
low.defvjp(low_keep, low_pass)
low_back.defvjp(back_keep, back_low)

def layer_norm(values, gain, shift):
    center = values - lax.optimization_barrier(jnp.mean(values, axis=-1, keepdims=True))
    spread = lax.optimization_barrier(jnp.mean(center * center, axis=-1, keepdims=True))
    return center * lax.rsqrt(spread + 1e-06) * gain + shift

def exact_gelu(values):
    return jax.nn.gelu(values, approximate=False)

def dot_high(left, right):
    return jnp.dot(left, right, precision=lax.Precision.HIGHEST, preferred_element_type=jnp.float32)

def reference(layer_in, scene_len, scene_group, scene_off, w_qkv, bias_q, bias_v, w_out, bias_out, w_up, bias_up, w_down, bias_down, gain_one, shift_one, gain_two, shift_two, grad_out):
    row_ids = jnp.arange(TOKENS, dtype=jnp.int32)
    owners = row_ids // CAPACITY
    places = row_ids % CAPACITY
    inside = (scene_group[None, :] == owners[:, None]) & (scene_off[None, :] <= places[:, None]) & (places[:, None] < (scene_off + scene_len)[None, :])
    labels = jnp.arange(1, SCENES + 1, dtype=jnp.int32)
    scene_id = lax.optimization_barrier(jnp.sum(jnp.where(inside, labels[None, :], 0), axis=1)).astype(jnp.int32).reshape(N_SCENE, CAPACITY)

    def forward(inputs, w_qkv, bias_q, bias_v, w_out, bias_out, w_up, bias_up, w_down, bias_down, gain_one, shift_one, gain_two, shift_two):

        def group_layer(carried):
            group_in, group_ids = carried
            allowed = group_ids[:, None] == group_ids[None, :]
            normed_one = low(layer_norm(group_in, gain_one, shift_one))
            qkv_bias = jnp.concatenate([bias_q, jnp.zeros((D,), jnp.float32), bias_v])
            qkv = low_back(low(dot_high(normed_one, w_qkv) + qkv_bias))
            split = qkv.reshape(CAPACITY, 3, HEADS, HEAD_DIM).transpose(1, 2, 0, 3)

            def attend(head_parts):
                query_head, key_head, value_head = head_parts
                scores = dot_high(query_head, key_head.T) * 0.125
                scores = low_back(jnp.where(allowed, scores, -1e+30))
                peak = lax.optimization_barrier(jnp.max(scores, axis=-1, keepdims=True))
                weights = jnp.exp(scores - peak)
                probs = low(weights / lax.optimization_barrier(jnp.sum(weights, axis=-1, keepdims=True)))
                return dot_high(probs, value_head)
            heads_out = lax.map(jax.checkpoint(attend), (split[0], split[1], split[2]))
            attended = low_back(low(heads_out.transpose(1, 0, 2).reshape(CAPACITY, D)))
            middle = group_in + low_back(dot_high(attended, w_out) + bias_out)
            normed_two = low(layer_norm(middle, gain_two, shift_two))
            activated = low(exact_gelu(low_back(dot_high(normed_two, w_up) + bias_up)))
            return middle + dot_high(activated, w_down) + bias_down
        outputs = lax.map(jax.checkpoint(group_layer), (inputs.reshape(N_SCENE, CAPACITY, D), scene_id))
        return outputs.reshape(TOKENS, D)
    result, back = jax.vjp(forward, layer_in.astype(jnp.float32), w_qkv.astype(jnp.float32), bias_q.astype(jnp.float32), bias_v.astype(jnp.float32), w_out.astype(jnp.float32), bias_out.astype(jnp.float32), w_up.astype(jnp.float32), bias_up.astype(jnp.float32), w_down.astype(jnp.float32), bias_down.astype(jnp.float32), gain_one.astype(jnp.float32), shift_one.astype(jnp.float32), gain_two.astype(jnp.float32), shift_two.astype(jnp.float32))
    grads = back(grad_out.astype(jnp.float32))
    return (result.astype(jnp.bfloat16), grads[0].astype(jnp.bfloat16), grads[1], grads[2], grads[3], grads[4], grads[5], grads[6], grads[7], grads[8], grads[9], grads[10], grads[11], grads[12], grads[13])
```

```python
import functools

import jax
import jax.numpy as jnp
import numpy as np
from jax import lax
from jax.experimental import pallas as pl
from jax.experimental.pallas import tpu as pltpu
from jax.sharding import PartitionSpec as P

HEAD_DIM = 64
PAIR = 2 * HEAD_DIM
EPS = 1e-06
NEG = -1e30
BF = jnp.bfloat16
F32 = jnp.float32


NT = (((1,), (1,)), ((), ()))
NN = (((1,), (0,)), ((), ()))


def dot(a, b, dims=NN):
    return lax.dot_general(a, b, dims, preferred_element_type=F32)


def split3(value):
    high = value.astype(BF)
    rest = value - high.astype(F32)
    middle = rest.astype(BF)
    low = (rest - middle.astype(F32)).astype(BF)
    return high, middle, low


def lanes_of(rows):
    return lax.broadcasted_iota(jnp.int32, (rows, PAIR), 1)


def forward_kernel(pairs, tile, first, q_ref, qkv_ref, fq_ref, fk_ref, out_ref, feat_ref, keys, vals):
    capacity = qkv_ref.shape[0]

    @pl.when(pl.program_id(0) == 0)
    def _():
        for p in range(pairs):
            base = 3 * PAIR * p
            keys[p, :, :PAIR] = qkv_ref[:, base + PAIR : base + 2 * PAIR]
            keys[p, :, PAIR:] = fk_ref[...]
            vals[p, :, :PAIR] = qkv_ref[:, base + 2 * PAIR : base + 3 * PAIR]
            vals[p, :, PAIR:] = jnp.ones((capacity, PAIR), BF)

    lane = lanes_of(tile)
    low_half = lane < HEAD_DIM
    marks = fq_ref[...]
    zero = jnp.zeros((), BF)
    for p in range(pairs):
        base = 3 * PAIR * p
        query = q_ref[:, base : base + PAIR] * jnp.asarray(0.125, BF)
        stacked = jnp.concatenate(
            [
                jnp.concatenate([jnp.where(low_half, query, zero), marks], 1),
                jnp.concatenate([jnp.where(low_half, zero, query), marks], 1),
            ],
            0,
        )
        scores = dot(stacked, keys[p], NT)
        peak = jnp.max(scores, axis=1, keepdims=True)
        weights = jnp.exp(scores - peak).astype(BF)
        sums = dot(weights, vals[p])
        total = sums[:, PAIR:]
        values = sums[:, :PAIR] / total
        out_ref[:, p * PAIR : (p + 1) * PAIR] = jnp.where(
            low_half, values[:tile], values[tile:]
        ).astype(BF)
        high, middle, low = split3(peak + jnp.log(total))
        for k in range(2):
            rows = slice(k * tile, (k + 1) * tile)
            kept = jnp.where(lane == 64, -high[rows], marks)
            kept = jnp.where(lane == 65, -middle[rows], kept)
            feat_ref[2 * p + k] = jnp.where(lane == 66, -low[rows], kept)


def attend(qkv, marks_q, marks_k, start, rows):
    capacity, width = qkv.shape
    pairs = width // (3 * PAIR)
    tile = 128
    first = start // tile
    return pl.pallas_call(
        functools.partial(forward_kernel, pairs, tile, first),
        grid=(rows // tile,),
        in_specs=[
            pl.BlockSpec((tile, width), lambda i: (first + i, 0)),
            pl.BlockSpec((capacity, width), lambda i: (0, 0)),
            pl.BlockSpec((tile, PAIR), lambda i: (first + i, 0)),
            pl.BlockSpec((capacity, PAIR), lambda i: (0, 0)),
        ],
        out_specs=[
            pl.BlockSpec((tile, pairs * PAIR), lambda i: (i, 0)),
            pl.BlockSpec((2 * pairs, tile, PAIR), lambda i: (0, i, 0)),
        ],
        out_shape=[
            jax.ShapeDtypeStruct((rows, pairs * PAIR), BF),
            jax.ShapeDtypeStruct((2 * pairs, rows, PAIR), BF),
        ],
        scratch_shapes=[
            pltpu.VMEM((pairs, capacity, 2 * PAIR), BF),
            pltpu.VMEM((pairs, capacity, 2 * PAIR), BF),
        ],
        compiler_params=pltpu.CompilerParams(vmem_limit_bytes=56 << 20),
        name="attend",
    )(qkv, qkv, marks_q, marks_k)


def backward_kernel(tq, tk, qkv_ref, feat_ref, fk_ref, out_ref, grad_ref, res_ref, keys, vals, keys_t, dk, dv):
    capacity = qkv_ref.shape[0]
    lane_all = lanes_of(capacity)
    key = qkv_ref[:, PAIR : 2 * PAIR]
    keys[:, :PAIR] = key
    keys[:, PAIR:] = fk_ref[...]
    vals[:, :PAIR] = qkv_ref[:, 2 * PAIR :]
    vals[:, PAIR:] = jnp.where(lane_all < 3, 1.0, 0.0).astype(BF)
    wide = key.astype(F32)
    keys_t[...] = (wide - jnp.mean(wide, axis=0, keepdims=True)).T.astype(BF)
    dk[...] = jnp.zeros_like(dk)
    dv[...] = jnp.zeros_like(dv)
    lane = lanes_of(tq)
    low_half = lane < HEAD_DIM
    zero = jnp.zeros((), BF)

    def query_step(i, carry):
        rows = pl.ds(pl.multiple_of(i * tq, tq), tq)
        query = qkv_ref[rows, :PAIR] * jnp.asarray(0.125, BF)
        grad = grad_ref[rows, :]
        product = grad.astype(F32) * out_ref[rows, :].astype(F32)
        masked_q, masked_g, marks_g = [], [], []
        for k in range(2):
            mine = low_half if k == 0 else jnp.logical_not(low_half)
            masked_q.append(jnp.where(mine, query, zero))
            masked_g.append(jnp.where(mine, grad, zero))
            delta = jnp.sum(jnp.where(mine, product, 0.0), axis=1, keepdims=True)
            high, middle, low = split3(jnp.broadcast_to(delta, (tq, PAIR)))
            mark = jnp.where(lane == 0, -high, zero)
            mark = jnp.where(lane == 1, -middle, mark)
            marks_g.append(jnp.where(lane == 2, -low, mark))
        q_plain = jnp.concatenate(masked_q, 0)
        g_plain = jnp.concatenate(masked_g, 0)
        q_full = jnp.concatenate(
            [q_plain, jnp.concatenate([feat_ref[0, rows, :], feat_ref[1, rows, :]], 0)], 1
        )
        g_full = jnp.concatenate([g_plain, jnp.concatenate(marks_g, 0)], 1)

        dq_t = jnp.zeros((PAIR, 2 * tq), F32)
        for j in range(capacity // tk):
            cols = slice(j * tk, (j + 1) * tk)
            probs = jnp.exp(dot(keys[cols, :], q_full, NT))
            centered = dot(vals[cols, :], g_full, NT)
            dv[cols, :] += dot(probs.astype(BF), g_plain)
            score_grad = (probs * centered).astype(BF)
            dk[cols, :] += dot(score_grad, q_plain)
            dq_t = dq_t + dot(keys_t[:, cols], score_grad)
        merged = jnp.concatenate([dq_t[:HEAD_DIM, :tq], dq_t[HEAD_DIM:, tq:]], 0)
        res_ref[rows, :PAIR] = (merged * 0.125).T.astype(BF)
        return carry

    lax.fori_loop(0, capacity // tq, query_step, 0)
    res_ref[:, PAIR : 2 * PAIR] = dk[...].astype(BF)
    res_ref[:, 2 * PAIR :] = dv[...].astype(BF)


def attend_back(p, qkv, feats, marks_k, attended, grads):
    capacity = qkv.shape[0]
    tq = 256
    tk = 512
    return pl.pallas_call(
        functools.partial(backward_kernel, tq, tk),
        grid=(1,),
        in_specs=[
            pl.BlockSpec((capacity, 3 * PAIR), lambda i: (0, p)),
            pl.BlockSpec((2, capacity, PAIR), lambda i: (p, 0, 0)),
            pl.BlockSpec((capacity, PAIR), lambda i: (0, 0)),
            pl.BlockSpec((capacity, PAIR), lambda i: (0, p)),
            pl.BlockSpec((capacity, PAIR), lambda i: (0, p)),
        ],
        out_specs=pl.BlockSpec((capacity, 3 * PAIR), lambda i: (0, 0)),
        out_shape=jax.ShapeDtypeStruct((capacity, 3 * PAIR), BF),
        scratch_shapes=[
            pltpu.VMEM((capacity, 2 * PAIR), BF),
            pltpu.VMEM((capacity, 2 * PAIR), BF),
            pltpu.VMEM((PAIR, capacity), BF),
            pltpu.VMEM((capacity, PAIR), F32),
            pltpu.VMEM((capacity, PAIR), F32),
        ],
        compiler_params=pltpu.CompilerParams(vmem_limit_bytes=56 << 20),
        name="attend_back",
    )(qkv, feats, marks_k, attended, grads)


def feed_kernel(
    normed_ref, grad_ref, up_ref, bias_ref, down_ref,
    out_ref, e_ref, up_t_ref, down_t_ref, bias_grad_ref, out_acc, e_acc, grad_t,
):
    step = pl.program_id(0)

    @pl.when(step == 0)
    def _():
        out_acc[...] = jnp.zeros_like(out_acc)
        e_acc[...] = jnp.zeros_like(e_acc)
        grad_t[...] = grad_ref[...].astype(F32).T.astype(BF)

    pre = dot(normed_ref[...], up_ref[...]) + bias_ref[...]
    cdf = 0.5 * (1.0 + lax.erf(pre * np.float32(0.5**0.5)))
    active = (pre * cdf).astype(BF)
    slope = cdf + pre * jnp.exp(pre * pre * -0.5) * np.float32(0.3989422804014327)
    out_acc[...] += dot(active, down_ref[...])
    pre_grad = slope * dot(grad_ref[...], down_ref[...], NT)
    low = pre_grad.astype(BF)
    e_acc[...] += dot(low, up_ref[...], NT)
    down_t_ref[...] = dot(grad_t[...], active).astype(BF)
    up_t_ref[...] = dot(pre_grad.T.astype(BF), normed_ref[...]).astype(BF)
    bias_grad_ref[...] = jnp.sum(low.astype(F32), axis=0, keepdims=True)

    @pl.when(step == pl.num_programs(0) - 1)
    def _():
        out_ref[...] = out_acc[...]
        e_ref[...] = e_acc[...]


def feed(normed, grad_out, w_up, bias_up, w_down):
    rows, d = normed.shape
    ff = w_up.shape[1]
    tile = 512
    whole = pl.BlockSpec((rows, d), lambda i: (0, 0))
    return pl.pallas_call(
        feed_kernel,
        grid=(ff // tile,),
        in_specs=[
            whole,
            whole,
            pl.BlockSpec((d, tile), lambda i: (0, i)),
            pl.BlockSpec((1, tile), lambda i: (0, i)),
            pl.BlockSpec((tile, d), lambda i: (i, 0)),
        ],
        out_specs=[
            whole,
            whole,
            pl.BlockSpec((tile, d), lambda i: (i, 0)),
            pl.BlockSpec((d, tile), lambda i: (0, i)),
            pl.BlockSpec((1, tile), lambda i: (0, i)),
        ],
        out_shape=[
            jax.ShapeDtypeStruct((rows, d), F32),
            jax.ShapeDtypeStruct((rows, d), F32),
            jax.ShapeDtypeStruct((ff, d), BF),
            jax.ShapeDtypeStruct((d, ff), BF),
            jax.ShapeDtypeStruct((1, ff), F32),
        ],
        scratch_shapes=[
            pltpu.VMEM((rows, d), F32),
            pltpu.VMEM((rows, d), F32),
            pltpu.VMEM((d, rows), BF),
        ],
        compiler_params=pltpu.CompilerParams(vmem_limit_bytes=56 << 20),
        name="feed",
    )(normed, grad_out, w_up, bias_up.astype(F32)[None], w_down)


def order_kernel(index_ref, in_ref, out_ref):
    out_ref[...] = in_ref[...]


def order_columns(matrix, index):
    rows, columns = matrix.shape
    count = columns // PAIR
    return pl.pallas_call(
        order_kernel,
        grid_spec=pltpu.PrefetchScalarGridSpec(
            num_scalar_prefetch=1,
            grid=(count,),
            in_specs=[pl.BlockSpec((rows, PAIR), lambda i, index: (0, index[i]))],
            out_specs=pl.BlockSpec((rows, PAIR), lambda i, index: (0, i)),
        ),
        out_shape=jax.ShapeDtypeStruct(matrix.shape, matrix.dtype),
        name="order_columns",
    )(index, matrix)


def swap(value, axis, bit):
    size = lax.axis_size(axis)
    return lax.ppermute(value, axis, [(i, i ^ bit) for i in range(size)])


def gather_head(value, size):
    chunks = [value]
    for r in range(1, size):
        low = r & -r
        chunks.append(swap(chunks[r ^ low], "head", low))
    return chunks


def halve(blocks, axis, position, bit):
    mine = (lax.axis_index(axis) // bit) % 2
    kept = lax.dynamic_index_in_dim(blocks, mine, position, keepdims=False)
    sent = lax.dynamic_index_in_dim(blocks, 1 - mine, position, keepdims=False)
    got = swap(sent, axis, bit)
    return (kept.astype(F32) + got.astype(F32)).astype(blocks.dtype)


def scatter_axis(blocks, axis, position):
    size = blocks.shape[position]
    bit = 1
    while bit < size:
        shape = blocks.shape
        split = shape[:position] + (shape[position] // 2, 2) + shape[position + 1 :]
        blocks = halve(blocks.reshape(split), axis, position + 1, bit)
        bit *= 2
    return blocks.reshape(blocks.shape[:position] + blocks.shape[position + 1 :])


def scatter_all(value, scenes, heads):
    blocks = value.reshape((scenes, heads, value.shape[0] // (scenes * heads)) + value.shape[1:])
    return scatter_axis(scatter_axis(blocks, "head", 1), "scene", 0)


@functools.lru_cache
def unit_plan(d, scenes, heads):
    total = scenes * heads
    block = 3 * d // total
    width = d // heads
    unit = int(np.gcd(block, min(width, PAIR)))
    pairs = width // PAIR
    count = 3 * width // unit
    per_slot = count // scenes
    order = np.zeros((heads, count), np.int32)
    edges = []
    for g in range(heads):
        room = [[] for _ in range(scenes)]
        later = []
        for u in range(count):
            row = u * unit
            p, rest = divmod(row, 3 * PAIR)
            part, offset = divmod(rest, PAIR)
            target = part * d + g * width + p * PAIR + offset
            owner, place = divmod(target, block)
            entry = (u, owner, place // unit)
            slot = room[owner // heads]
            if len(slot) < per_slot:
                slot.append(entry)
            else:
                later.append(entry)
        for entry in later:
            next(slot for slot in room if len(slot) < per_slot).append(entry)
        for s in range(scenes):
            for k, (u, owner, place) in enumerate(room[s]):
                order[g, s * per_slot + k] = u
                edges.append((s * heads + g, owner, k, place))
    rounds = []
    left = list(edges)
    while left:
        by_source = {}
        for e in left:
            by_source.setdefault(e[0], []).append(e)
        match = {}

        def place_one(source, seen):
            for e in by_source[source]:
                if e[1] in seen:
                    continue
                seen.add(e[1])
                if e[1] not in match or place_one(match[e[1]][0], seen):
                    match[e[1]] = e
                    return True
            return False

        for source in range(total):
            place_one(source, set())
        chosen = sorted(match.values())
        rounds.append(chosen)
        taken = set(chosen)
        left = [e for e in left if e not in taken]
    return unit, per_slot, order, rounds


def own_rows(product, d, scenes, heads):
    unit, per_slot, order, rounds = unit_plan(d, scenes, heads)
    columns = product.shape[1]
    mine = jnp.asarray(order)[lax.axis_index("head")]
    units = product.reshape(-1, unit, columns)
    ordered = jnp.take(units, mine, axis=0).reshape(scenes, per_slot * unit, columns)
    summed = scatter_axis(ordered, "scene", 0).reshape(per_slot, unit, columns)
    me = lax.axis_index("scene") * heads + lax.axis_index("head")
    result = jnp.zeros((per_slot, unit, columns), summed.dtype)
    for chosen in rounds:
        source = np.zeros(scenes * heads, np.int32)
        target = np.zeros(scenes * heads, np.int32)
        for a, b, k, place in chosen:
            source[a] = k
            target[b] = place
        sent = lax.dynamic_index_in_dim(summed, jnp.asarray(source)[me], 0, keepdims=True)
        got = lax.ppermute(sent, ("scene", "head"), [(a, b) for a, b, _, _ in chosen])
        result = lax.dynamic_update_slice_in_dim(result, got, jnp.asarray(target)[me], 0)
    return result.reshape(per_slot * unit, columns)


def norm_parts(values):
    center = values - jnp.mean(values, axis=-1, keepdims=True)
    spread = jnp.mean(center * center, axis=-1, keepdims=True)
    scale = lax.rsqrt(spread + EPS)
    return center * scale, scale


def norm_back(xhat, scale, gain, e):
    hat = e * gain
    return scale * (
        hat
        - jnp.mean(hat, axis=-1, keepdims=True)
        - xhat * jnp.mean(hat * xhat, axis=-1, keepdims=True)
    )


def scene_ids(scene_len, scene_group, scene_off, owner, places):
    inside = (
        (scene_group[None, :] == owner)
        & (scene_off[None, :] <= places[:, None])
        & (places[:, None] < (scene_off + scene_len)[None, :])
    )
    labels = jnp.arange(1, scene_len.shape[0] + 1, dtype=jnp.int32)
    return jnp.sum(jnp.where(inside, labels[None, :], 0), axis=1)


def on_device(
    layer_in, scene_len, scene_group, scene_off, w_qkv, bias_q, bias_v, w_out, bias_out,
    w_up, bias_up, w_down, bias_down, gain_one, shift_one, gain_two, shift_two, grad_out,
):
    rows, d = layer_in.shape
    ff = w_up.shape[1]
    heads = lax.axis_size("head")
    scenes = lax.axis_size("scene")
    total = heads * scenes
    width = d // heads
    pairs = width // PAIR
    capacity = rows * heads
    h = lax.axis_index("head")
    g_one, s_one, g_two, s_two = (v.astype(F32) for v in (gain_one, shift_one, gain_two, shift_two))

    chunks = gather_head(layer_in, heads)

    peers = jnp.arange(heads, dtype=jnp.int32) ^ h
    index = (
        peers[:, None, None] * pairs
        + jnp.arange(pairs, dtype=jnp.int32)[None, :, None]
        + jnp.arange(3, dtype=jnp.int32)[None, None, :] * (d // PAIR)
    ).reshape(-1)
    w_rel = order_columns(w_qkv, index)
    own_q = lax.dynamic_slice_in_dim(bias_q.astype(F32), h * width, width).reshape(pairs, 1, PAIR)
    own_v = lax.dynamic_slice_in_dim(bias_v.astype(F32), h * width, width).reshape(pairs, 1, PAIR)
    own_bias = jnp.concatenate([own_q, jnp.zeros_like(own_q), own_v], 1).reshape(-1)
    places = (peers[:, None] * rows + jnp.arange(rows, dtype=jnp.int32)[None]).reshape(-1)
    ids = scene_ids(scene_len, scene_group, scene_off, lax.axis_index("scene"), places)
    lane = jnp.arange(PAIR, dtype=jnp.int32)[None, :]
    same = ids[:, None] == lane
    marks_q = same.astype(BF)
    marks_k = jnp.where(
        lane < HEAD_DIM, jnp.where(same, 0.0, NEG), jnp.where(lane < HEAD_DIM + 3, 1.0, 0.0)
    ).astype(BF)

    inputs = layer_in.astype(F32)
    group = jnp.concatenate(chunks, 0).astype(F32)
    normed_one = (norm_parts(group)[0] * g_one + s_one).astype(BF)
    qkv = (dot(normed_one, w_rel[:, : 3 * width]) + own_bias).astype(BF)

    half = capacity // 2
    far_out, far_feat = attend(qkv, marks_q, marks_k, half, half)
    near_out, near_feat = attend(qkv, marks_q, marks_k, 0, half)
    own_out = jnp.concatenate([near_out, far_out], 0)
    feats = jnp.concatenate([near_feat, far_feat], 1)
    parts = []
    for r in range(heads):
        source = far_out if r >= heads // 2 else near_out
        at = (r % (heads // 2)) * rows
        part = source[at : at + rows]
        parts.append(part if r == 0 else swap(part, "head", r))
    stacked = jnp.stack(parts)
    attended = jnp.concatenate(
        [lax.dynamic_index_in_dim(stacked, peers[k], 0, keepdims=False) for k in range(heads)], 1
    )

    middle = inputs + dot(attended, w_out) + bias_out.astype(F32)
    hat_two, scale_two = norm_parts(middle)
    normed_two = (hat_two * g_two + s_two).astype(BF)
    forward, e_two, up_t, down_t, grad_bias_up = feed(normed_two, grad_out, w_up, bias_up, w_down)
    layer_out = (middle + forward + bias_down.astype(F32)).astype(BF)
    grad_w_up = scatter_all(up_t, scenes, heads)
    grad_w_down = scatter_all(down_t, scenes, heads)

    grad_middle = grad_out.astype(F32) + norm_back(hat_two, scale_two, g_two, e_two)
    grad_gain_two = jnp.sum(e_two * hat_two, axis=0)
    grad_shift_two = jnp.sum(e_two, axis=0)
    branch_grad = grad_middle.astype(BF)
    grad_bias_out = jnp.sum(branch_grad.astype(F32), axis=0)
    grad_bias_down = jnp.sum(grad_out.astype(F32), axis=0)
    attended_grad = dot(branch_grad, w_out, NT).astype(BF)
    out_t = lax.dot_general(
        branch_grad, attended, (((0,), (0,)), ((), ())), preferred_element_type=F32
    ).astype(BF)
    grad_w_out = scatter_all(out_t, scenes, heads)

    pieces = []
    for r in range(heads):
        piece = lax.dynamic_slice_in_dim(attended_grad, peers[r] * width, width, 1)
        pieces.append(piece if r == 0 else swap(piece, "head", r))
    head_grads = jnp.concatenate(pieces, 0)

    grads, e_parts, sums = [], [], []
    for p in range(pairs):
        pair_grad = attend_back(p, qkv, feats, marks_k, own_out, head_grads)
        grads.append(pair_grad)
        for r in range(heads):
            piece = pair_grad[r * rows : (r + 1) * rows]
            e_parts.append((r, p, piece if r == 0 else swap(piece, "head", r)))
    product = lax.dot_general(
        jnp.concatenate(grads, 1), normed_one, (((0,), (0,)), ((), ())), preferred_element_type=F32
    ).astype(BF)
    grad_w_qkv = own_rows(product, d, scenes, heads)

    token_grads = jnp.concatenate([piece for _, _, piece in sorted(e_parts, key=lambda e: e[:2])], 1)
    e_one = dot(token_grads, w_rel, NT)
    hat_one, scale_one = norm_parts(inputs)
    grad_in = (grad_middle + norm_back(hat_one, scale_one, g_one, e_one)).astype(BF)
    grad_gain_one = jnp.sum(e_one * hat_one, axis=0)
    grad_shift_one = jnp.sum(e_one, axis=0)
    column_sums = jnp.sum(token_grads.astype(F32), axis=0).reshape(heads, pairs, 3, PAIR)
    by_head = jnp.concatenate(
        [lax.dynamic_index_in_dim(column_sums, peers[k], 0) for k in range(heads)], 0
    )

    vectors = [
        by_head[:, :, 0].reshape(-1), by_head[:, :, 2].reshape(-1), grad_bias_out,
        grad_bias_up.reshape(-1), grad_bias_down, grad_gain_one, grad_shift_one,
        grad_gain_two, grad_shift_two,
    ]
    packed = jnp.concatenate([v.reshape(total, -1) for v in vectors], 1)
    packed = scatter_all(packed, scenes, heads).reshape(-1)
    small, at = [], 0
    for v in vectors:
        size = v.shape[0] // total
        small.append(packed[at : at + size])
        at += size
    return (
        layer_out,
        grad_in,
        grad_w_qkv.astype(F32).T,
        small[0],
        small[1],
        grad_w_out.reshape(-1, d).astype(F32).T,
        small[2],
        grad_w_up.reshape(-1, d).astype(F32).T,
        small[3],
        grad_w_down.reshape(-1, ff).astype(F32).T,
        small[4],
        small[5],
        small[6],
        small[7],
        small[8],
    )


def solution(mesh):
    rows, whole, part = P(("scene", "head"), None), P(), P(("scene", "head"))
    columns = P(None, ("scene", "head"))
    return jax.shard_map(
        on_device,
        mesh=mesh,
        in_specs=(rows,) + (whole,) * 16 + (rows,),
        out_specs=(
            rows, rows, columns, part, part, columns, part, columns, part, columns,
            part, part, part, part, part,
        ),
        check_vma=False,
    )
```

```python
import functools

import jax
import jax.numpy as jnp
import numpy as np
from jax import lax
from jax.experimental import pallas as pl
from jax.experimental.pallas import tpu as pltpu
from jax.sharding import PartitionSpec as P

HEAD_DIM = 64
PAIR = 2 * HEAD_DIM
EPS = 1e-06
NEG = -1e30
BF = jnp.bfloat16
F32 = jnp.float32
LIMIT = 58 << 20


NT = (((1,), (1,)), ((), ()))
NN = (((1,), (0,)), ((), ()))


def dot(a, b, dims=NN):
    return lax.dot_general(a, b, dims, preferred_element_type=F32)


def split3(value):
    high = value.astype(BF)
    rest = value - high.astype(F32)
    middle = rest.astype(BF)
    low = (rest - middle.astype(F32)).astype(BF)
    return high, middle, low


def lanes_of(rows):
    return lax.broadcasted_iota(jnp.int32, (rows, PAIR), 1)


def norm_parts(values):
    center = values - jnp.mean(values, axis=-1, keepdims=True)
    spread = jnp.mean(center * center, axis=-1, keepdims=True)
    scale = lax.rsqrt(spread + EPS)
    return center * scale, scale


def norm_back(xhat, scale, gain, e):
    hat = e * gain
    return scale * (
        hat
        - jnp.mean(hat, axis=-1, keepdims=True)
        - xhat * jnp.mean(hat * xhat, axis=-1, keepdims=True)
    )


def column_sum(value):
    return jnp.sum(value, axis=0, keepdims=True)


def transposed(value):
    return value.astype(F32).T.astype(BF)


def params():
    return pltpu.CompilerParams(vmem_limit_bytes=LIMIT)


def shape(dims, kind):
    return jax.ShapeDtypeStruct(dims, kind)


ANY = pl.BlockSpec(memory_space=pl.ANY)


def bits_below(size, start):
    bits = []
    while start < size:
        bits.append(start)
        start *= 2
    return bits


class Plan:
    def __init__(self, d, ff, scenes, heads):
        self.d, self.ff, self.scenes, self.heads = d, ff, scenes, heads
        self.total = scenes * heads
        scene_bits, head_bits = bits_below(scenes, 1), bits_below(heads, 2)
        self.outer = [("scene", b) for b in scene_bits[:2]]
        self.inner = [("head", b) for b in head_bits] + [("scene", b) for b in scene_bits[2:]]
        self.up_stages = self.outer + self.inner
        self.down_stages = self.outer[::-1] + self.inner
        self.out_stages = [("head", 1)] + self.up_stages
        self.qkv_stages = [("scene", b) for b in scene_bits]
        self.tiles = 2 ** len(self.outer)
        self.subs = 2 ** len(self.inner)
        self.block = ff // self.total

    def place(self, s, h, stages):
        value = 0
        for axis, bit in stages:
            value = 2 * value + int(bool((s if axis == "scene" else h) & bit))
        return value

    def owners(self, stages):
        found = {}
        for s in range(self.scenes):
            for h in range(self.heads):
                where = self.place(s, h, stages)
                if where not in found:
                    found[where] = (s, h)
        return [found[k] for k in range(len(found))]

    def units(self, stages):
        return [self.place(u // self.heads, u % self.heads, stages) for u in range(self.total)]


@functools.lru_cache
def unit_plan(d, scenes, heads):
    total = scenes * heads
    block = 3 * d // total
    width = d // heads
    unit = int(np.gcd(block, min(width, PAIR)))
    count = 3 * width // unit
    per_slot = count // scenes
    where = np.zeros((heads, count, 2), np.int32)
    edges = []
    for g in range(heads):
        room = [[] for _ in range(scenes)]
        later = []
        for u in range(count):
            row = u * unit
            p, rest = divmod(row, 3 * PAIR)
            part, offset = divmod(rest, PAIR)
            target = part * d + g * width + p * PAIR + offset
            owner, place = divmod(target, block)
            entry = (u, owner, place // unit)
            slot = room[owner // heads]
            if len(slot) < per_slot:
                slot.append(entry)
            else:
                later.append(entry)
        for entry in later:
            next(slot for slot in room if len(slot) < per_slot).append(entry)
        for s in range(scenes):
            for k, (u, owner, place) in enumerate(room[s]):
                where[g, u] = s, k
                edges.append((s * heads + g, owner, k, place))
    rounds = []
    left = list(edges)
    while left:
        by_source = {}
        for e in left:
            by_source.setdefault(e[0], []).append(e)
        match = {}

        def place_one(source, seen):
            for e in by_source[source]:
                if e[1] in seen:
                    continue
                seen.add(e[1])
                if e[1] not in match or place_one(match[e[1]][0], seen):
                    match[e[1]] = e
                    return True
            return False

        for source in range(total):
            place_one(source, set())
        chosen = sorted(match.values())
        rounds.append(chosen)
        taken = set(chosen)
        left = [e for e in left if e not in taken]
    return unit, per_slot, where, rounds


SCENE, HEAD, CORE, TILE, SUB, DOWN, OUT, QKV = range(8)


def number_table(plan):
    _, per_slot, where, _ = unit_plan(plan.d, plan.scenes, plan.heads)
    rows = []
    for s in range(plan.scenes):
        for h in range(plan.heads):
            row = [
                s, h, h & 1, plan.place(s, h, plan.outer), plan.place(s, h, plan.inner),
                plan.place(s, h, plan.down_stages + [("head", 1)]), plan.place(s, h, plan.out_stages),
            ]
            mine = plan.place(s, 0, plan.qkv_stages)
            for slot, k in where[h]:
                row.append((plan.place(int(slot), 0, plan.qkv_stages) ^ mine) * per_slot + int(k))
            rows.append(row)
    return np.asarray(rows, np.int32)


def marks_kernel(slots, rows, me, lens, groups, offs, q_ref, k_ref):
    place = lax.broadcasted_iota(jnp.int32, (rows, PAIR), 0) + (me[HEAD] ^ pl.program_id(0)) * rows

    def add(j, ids):
        inside = (place >= offs[j]) & (place < offs[j] + lens[j])
        return ids + jnp.where(inside, jnp.where(groups[j] == me[SCENE], j + 1, 0), 0)

    ids = lax.fori_loop(0, slots, add, jnp.zeros((rows, PAIR), jnp.int32))
    lane = lanes_of(rows)
    same = ids == lane
    q_ref[...] = jnp.where(same, 1.0, 0.0).astype(BF)
    k_ref[...] = jnp.where(
        lane < HEAD_DIM, jnp.where(same, 0.0, NEG), jnp.where(lane < HEAD_DIM + 3, 1.0, 0.0)
    ).astype(BF)


def marks(me, scene_len, scene_group, scene_off, rows, heads):
    spec = pl.BlockSpec((rows, PAIR), lambda i, *_: (i, 0))
    return pl.pallas_call(
        functools.partial(marks_kernel, scene_len.shape[0], rows),
        grid_spec=pltpu.PrefetchScalarGridSpec(
            num_scalar_prefetch=4, grid=(heads,), in_specs=[], out_specs=[spec, spec]
        ),
        out_shape=[shape((rows * heads, PAIR), BF)] * 2,
        name="marks",
    )(me, scene_len, scene_group, scene_off)


def project_kernel(me, x0, x1, w_ref, b_ref, *rest):
    out_ref = rest[-1]
    rows = x0.shape[0]
    for k, x in enumerate((x0, x1)):
        out_ref[k * rows : (k + 1) * rows, :] = (dot(x[...], w_ref[...]) + b_ref[0]).astype(BF)


def project(me, j, x0, x1, w_qkv, bias, capacity, width, before):
    rows, d = x0.shape
    whole = pl.BlockSpec((rows, d), lambda i, me: (0, 0))
    per = d // width
    extra = [] if before is None else [before]
    return pl.pallas_call(
        project_kernel,
        grid_spec=pltpu.PrefetchScalarGridSpec(
            num_scalar_prefetch=1,
            grid=(3,),
            in_specs=[
                whole,
                whole,
                pl.BlockSpec((d, width), lambda i, me: (0, i * per + me[HEAD])),
                pl.BlockSpec((1, 1, width), lambda i, me: (i, 0, me[HEAD])),
            ]
            + [ANY] * len(extra),
            out_specs=pl.BlockSpec((2 * rows, width), lambda i, me: (j, i)),
        ),
        out_shape=shape((capacity, 3 * width), BF),
        input_output_aliases={5: 0} if extra else {},
        compiler_params=params(),
        name="project",
    )(me, x0, x1, w_qkv, bias, *extra)


def forward_kernel(pairs, tile, q_ref, qkv_ref, fq_ref, fk_ref, out_ref, feat_ref, keys, vals):
    capacity, width3 = qkv_ref.shape
    width = width3 // 3

    @pl.when(pl.program_id(0) == 0)
    def _():
        for p in range(pairs):
            at = PAIR * p
            keys[p, :, :PAIR] = qkv_ref[:, width + at : width + at + PAIR]
            keys[p, :, PAIR:] = fk_ref[...]
            vals[p, :, :PAIR] = qkv_ref[:, 2 * width + at : 2 * width + at + PAIR]
            vals[p, :, PAIR:] = jnp.ones((capacity, PAIR), BF)

    lane = lanes_of(tile)
    low_half = lane < HEAD_DIM
    own_marks = fq_ref[...]
    zero = jnp.zeros((), BF)
    for p in range(pairs):
        query = q_ref[:, p * PAIR : (p + 1) * PAIR] * jnp.asarray(0.125, BF)
        stacked = jnp.concatenate(
            [
                jnp.concatenate([jnp.where(low_half, query, zero), own_marks], 1),
                jnp.concatenate([jnp.where(low_half, zero, query), own_marks], 1),
            ],
            0,
        )
        scores = dot(stacked, keys[p], NT)
        peak = jnp.max(scores, axis=1, keepdims=True)
        weights = jnp.exp(scores - peak).astype(BF)
        sums = dot(weights, vals[p])
        total = sums[:, PAIR:]
        values = sums[:, :PAIR] / total
        out_ref[:, p * PAIR : (p + 1) * PAIR] = jnp.where(
            low_half, values[:tile], values[tile:]
        ).astype(BF)
        high, middle, low = split3(peak + jnp.log(total))
        for k in range(2):
            rows = slice(k * tile, (k + 1) * tile)
            kept = jnp.where(lane == 64, -high[rows], own_marks)
            kept = jnp.where(lane == 65, -middle[rows], kept)
            feat_ref[2 * p + k] = jnp.where(lane == 66, -low[rows], kept)


def attend(j, qkv, marks_q, marks_k, count):
    capacity, width3 = qkv.shape
    width = width3 // 3
    pairs = width // PAIR
    tile = 128
    first = j * count // tile
    return pl.pallas_call(
        functools.partial(forward_kernel, pairs, tile),
        grid=(count // tile,),
        in_specs=[
            pl.BlockSpec((tile, width), lambda i: (first + i, 0)),
            pl.BlockSpec((capacity, width3), lambda i: (0, 0)),
            pl.BlockSpec((tile, PAIR), lambda i: (first + i, 0)),
            pl.BlockSpec((capacity, PAIR), lambda i: (0, 0)),
        ],
        out_specs=[
            pl.BlockSpec((tile, width), lambda i: (i, 0)),
            pl.BlockSpec((2 * pairs, tile, PAIR), lambda i: (0, i, 0)),
        ],
        out_shape=[shape((count, width), BF), shape((2 * pairs, count, PAIR), BF)],
        scratch_shapes=[
            pltpu.VMEM((pairs, capacity, 2 * PAIR), BF),
            pltpu.VMEM((pairs, capacity, 2 * PAIR), BF),
        ],
        compiler_params=params(),
        name="attend",
    )(qkv, qkv, marks_q, marks_k)


def backward_kernel(tq, tk, first, last, olds, *refs):
    q_ref, k_ref, v_ref, fk_ref, feat_ref, out_ref, g0_ref, g1_ref = refs[:8]
    at = 8
    carried = ()
    if not first:
        carried = refs[at : at + 2]
        at += 2
    old_refs = refs[at : at + olds]
    at += olds
    scratch = 6
    outs = refs[at : len(refs) - scratch]
    keys, vals, keys_t, grads, dk, dv = refs[len(refs) - scratch :]
    capacity = k_ref.shape[0]
    rows = g0_ref.shape[0]
    count = q_ref.shape[0]
    lane_all = lanes_of(capacity)
    key = k_ref[...]
    keys[:, :PAIR] = key
    keys[:, PAIR:] = fk_ref[...]
    vals[:, :PAIR] = v_ref[...]
    vals[:, PAIR:] = jnp.where(lane_all < 3, 1.0, 0.0).astype(BF)
    wide = key.astype(F32)
    keys_t[...] = (wide - jnp.mean(wide, axis=0, keepdims=True)).T.astype(BF)
    grads[:rows] = g0_ref[...]
    grads[rows:] = g1_ref[...]
    if first:
        dk[...] = jnp.zeros_like(dk)
        dv[...] = jnp.zeros_like(dv)
    else:
        dk[...] = carried[0][...]
        dv[...] = carried[1][...]
    lane = lanes_of(tq)
    low_half = lane < HEAD_DIM
    zero = jnp.zeros((), BF)

    def query_step(i, carry):
        span = pl.ds(pl.multiple_of(i * tq, tq), tq)
        query = q_ref[span, :] * jnp.asarray(0.125, BF)
        grad = grads[span, :]
        product = grad.astype(F32) * out_ref[span, :].astype(F32)
        masked_q, masked_g, marks_g = [], [], []
        for k in range(2):
            mine = low_half if k == 0 else jnp.logical_not(low_half)
            masked_q.append(jnp.where(mine, query, zero))
            masked_g.append(jnp.where(mine, grad, zero))
            delta = jnp.sum(jnp.where(mine, product, 0.0), axis=1, keepdims=True)
            high, middle, low = split3(jnp.broadcast_to(delta, (tq, PAIR)))
            mark = jnp.where(lane == 0, -high, zero)
            mark = jnp.where(lane == 1, -middle, mark)
            marks_g.append(jnp.where(lane == 2, -low, mark))
        q_plain = jnp.concatenate(masked_q, 0)
        g_plain = jnp.concatenate(masked_g, 0)
        q_full = jnp.concatenate(
            [q_plain, jnp.concatenate([feat_ref[0, span, :], feat_ref[1, span, :]], 0)], 1
        )
        g_full = jnp.concatenate([g_plain, jnp.concatenate(marks_g, 0)], 1)

        dq_t = jnp.zeros((PAIR, 2 * tq), F32)
        for j in range(capacity // tk):
            cols = slice(j * tk, (j + 1) * tk)
            probs = jnp.exp(dot(keys[cols, :], q_full, NT))
            centered = dot(vals[cols, :], g_full, NT)
            dv[cols, :] += dot(probs.astype(BF), g_plain)
            score_grad = (probs * centered).astype(BF)
            dk[cols, :] += dot(score_grad, q_plain)
            dq_t = dq_t + dot(keys_t[:, cols], score_grad)
        merged = jnp.concatenate([dq_t[:HEAD_DIM, :tq], dq_t[HEAD_DIM:, tq:]], 0)
        grads[span, :] = (merged * 0.125).T.astype(BF)
        return carry

    lax.fori_loop(0, count // tq, query_step, 0)
    if last:
        for r, out in enumerate(outs):
            own = slice((r % 2) * rows, (r % 2 + 1) * rows)
            out[:, :PAIR] = old_refs[r // 2][own, :] if r // 2 < olds else grads[own, :]
            span = slice(r * rows, (r + 1) * rows)
            out[:, PAIR : 2 * PAIR] = dk[span, :].astype(BF)
            out[:, 2 * PAIR :] = dv[span, :].astype(BF)
    else:
        outs[0][...] = grads[...]
        outs[1][...] = dk[...]
        outs[2][...] = dv[...]


def attend_back(j, p, heads, qkv, feats, marks_k, attended, g0, g1, carried, olds):
    capacity, width3 = qkv.shape
    width = width3 // 3
    pairs = width // PAIR
    rows = g0.shape[0]
    count = 2 * rows
    first, last = j == 0, j == heads // 2 - 1
    tq, tk = 256, 512
    in_specs = [
        pl.BlockSpec((count, PAIR), lambda i: (j, p)),
        pl.BlockSpec((capacity, PAIR), lambda i: (0, pairs + p)),
        pl.BlockSpec((capacity, PAIR), lambda i: (0, 2 * pairs + p)),
        pl.BlockSpec((capacity, PAIR), lambda i: (0, 0)),
        pl.BlockSpec((2, count, PAIR), lambda i: (p, 0, 0)),
        pl.BlockSpec((count, PAIR), lambda i: (0, p)),
        pl.BlockSpec((rows, PAIR), lambda i: (0, p)),
        pl.BlockSpec((rows, PAIR), lambda i: (0, p)),
    ]
    whole = pl.BlockSpec((capacity, PAIR), lambda i: (0, 0))
    queries = pl.BlockSpec((count, PAIR), lambda i: (0, 0))
    args = [qkv, qkv, qkv, marks_k, feats, attended, g0, g1]
    if not first:
        in_specs += [whole, whole]
        args += list(carried)
    if last:
        in_specs += [queries] * len(olds)
        args += list(olds)
        chunk = pl.BlockSpec((rows, 3 * PAIR), lambda i: (0, 0))
        out_specs = [chunk] * heads
        out_shape = [shape((rows, 3 * PAIR), BF)] * heads
    else:
        out_specs = [queries, whole, whole]
        out_shape = [shape((count, PAIR), BF)] + [shape((capacity, PAIR), F32)] * 2
    return pl.pallas_call(
        functools.partial(backward_kernel, tq, tk, first, last, len(olds) if last else 0),
        grid=(1,),
        in_specs=in_specs,
        out_specs=out_specs,
        out_shape=out_shape,
        scratch_shapes=[
            pltpu.VMEM((capacity, 2 * PAIR), BF),
            pltpu.VMEM((capacity, 2 * PAIR), BF),
            pltpu.VMEM((PAIR, capacity), BF),
            pltpu.VMEM((count, PAIR), BF),
            pltpu.VMEM((capacity, PAIR), F32),
            pltpu.VMEM((capacity, PAIR), F32),
        ],
        compiler_params=params(),
        name="attend_back",
    )(*args)


def merge_kernel(heads, me, *refs):
    pieces, weights = refs[:heads], refs[heads : 2 * heads]
    own_ref, other_ref, bias_ref, gain_ref, shift_ref, middle_ref, normed_ref = refs[2 * heads :]
    half = pl.program_id(0)
    total = jnp.where(half == 0, own_ref[...], other_ref[...]).astype(F32) + bias_ref[...]
    for piece, weight in zip(pieces, weights):
        total = total + dot(piece[...], weight[...])
    hat, _ = norm_parts(total)
    normed_ref[...] = (hat * gain_ref[...] + shift_ref[...]).astype(BF)

    @pl.when(half == 0)
    def _():
        middle_ref[...] = total


def merge(me, pieces, w_out, own, other, bias, gain, shift):
    rows, d = own.shape
    heads = len(pieces)
    width = d // heads
    whole = pl.BlockSpec((rows, d), lambda i, me: (0, 0))
    row = pl.BlockSpec((1, d), lambda i, me: (0, 0))

    def weight(r):
        return pl.BlockSpec((width, d), lambda i, me: (me[HEAD] ^ r, 0))

    mine = pl.BlockSpec((rows, width), lambda i, me: (i, 0))
    theirs = pl.BlockSpec((rows, width), lambda i, me: (1 - i, 0))
    return pl.pallas_call(
        functools.partial(merge_kernel, heads),
        grid_spec=pltpu.PrefetchScalarGridSpec(
            num_scalar_prefetch=1,
            grid=(2,),
            in_specs=[theirs if r % 2 else mine for r in range(heads)]
            + [weight(r) for r in range(heads)]
            + [whole, whole, row, row, row],
            out_specs=[whole, pl.BlockSpec((rows, d), lambda i, me: (i, 0))],
        ),
        out_shape=[shape((rows, d), F32), shape((2 * rows, d), BF)],
        compiler_params=params(),
        name="merge",
    )(me, *pieces, *[w_out] * heads, own, other, bias, gain, shift)


def middle_kernel(heads, me, e_ref, more_ref, middle_ref, grad_ref, gain_ref, *refs):
    weights = refs[:heads]
    grad_middle_ref, branch_ref = refs[heads : heads + 2]
    pieces = refs[heads + 2 : 2 * heads + 2]
    sums_ref = refs[-1]
    e = e_ref[...] + more_ref[...].astype(F32)
    hat, scale = norm_parts(middle_ref[...])
    grad = grad_ref[...].astype(F32)
    total = grad + norm_back(hat, scale, gain_ref[...], e)
    low = total.astype(BF)
    grad_middle_ref[...] = total
    branch_ref[...] = low
    for piece, weight in zip(pieces, weights):
        piece[...] = dot(low, weight[...], NT).astype(BF)

    @pl.when(pl.program_id(0) == 0)
    def _():
        sums_ref[...] = jnp.zeros_like(sums_ref)

    for k, v in enumerate((low.astype(F32), grad, e * hat, e)):
        sums_ref[k : k + 1] += column_sum(v)


def middle_back(me, e, more, middle, grad_out, gain, w_out, heads):
    rows, d = middle.shape
    width = d // heads
    tile = 128
    block = pl.BlockSpec((tile, d), lambda i, me: (i, 0))

    def weight(r):
        return pl.BlockSpec((width, d), lambda i, me: (me[HEAD] ^ r, 0))

    return pl.pallas_call(
        functools.partial(middle_kernel, heads),
        grid_spec=pltpu.PrefetchScalarGridSpec(
            num_scalar_prefetch=1,
            grid=(rows // tile,),
            in_specs=[block] * 4
            + [pl.BlockSpec((1, d), lambda i, me: (0, 0))]
            + [weight(r) for r in range(heads)],
            out_specs=[block, block]
            + [pl.BlockSpec((tile, width), lambda i, me: (i, 0))] * heads
            + [pl.BlockSpec((4, d), lambda i, me: (0, 0))],
        ),
        out_shape=[shape((rows, d), F32), shape((rows, d), BF)]
        + [shape((rows, width), BF)] * heads
        + [shape((4, d), F32)],
        compiler_params=params(),
        name="middle_back",
    )(me, e, more, middle, grad_out, gain, *[w_out] * heads)


def out_grad_kernel(places, me, branch_ref, *refs):
    pieces, out_ref = refs[:-1], refs[-1]
    count = len(places)
    unit = branch_ref.shape[1] // count
    turned = transposed(branch_ref[...])
    for r, piece in enumerate(pieces):
        value = dot(turned, piece[...]).astype(BF)
        column = me[HEAD] ^ r
        for u in range(count):
            out_ref[me[OUT] ^ places[u], column] = value[u * unit : (u + 1) * unit]


def out_grad(me, plan, branch, pieces):
    rows, d = branch.shape
    heads = len(pieces)
    width = d // heads
    dims = (plan.total, heads, d // plan.total, width)
    return pl.pallas_call(
        functools.partial(out_grad_kernel, plan.units(plan.out_stages)),
        grid_spec=pltpu.PrefetchScalarGridSpec(
            num_scalar_prefetch=1,
            grid=(1,),
            in_specs=[pl.BlockSpec((rows, d), lambda i, me: (0, 0))]
            + [pl.BlockSpec((rows, width), lambda i, me, r=r: (r % 2, 0)) for r in range(heads)],
            out_specs=pl.BlockSpec(dims, lambda i, me: (0, 0, 0, 0)),
        ),
        out_shape=shape(dims, BF),
        compiler_params=params(),
        name="out_grad",
    )(me, branch, *pieces)


def feed_kernel(plan, split, me, *refs):
    normed_ref, g0_ref, g1_ref = refs[:3]
    ups, biases, downs = (refs[3 + k * split : 3 + (k + 1) * split] for k in range(3))
    (
        out_ref, out_other_ref, e_ref, e_other_ref, up_kept, up_sent, down_kept, down_sent, bias_grad_ref,
        out_acc, e_acc, grad_t, up, down, active_all, low_t,
    ) = refs[3 + 3 * split :]
    step = pl.program_id(0)
    rows, d = g0_ref.shape
    tile = up.shape[1]
    sub = tile // split
    unit = d // plan.total

    @pl.when(step == 0)
    def _():
        out_ref[...] = jnp.zeros_like(out_ref)
        e_ref[...] = jnp.zeros_like(e_ref)
        out_acc[...] = jnp.zeros_like(out_acc)
        e_acc[...] = jnp.zeros_like(e_acc)
        places = plan.units(plan.down_stages + [("head", 1)])
        for k, ref in enumerate((g0_ref, g1_ref)):
            turned = transposed(ref[...])
            for u in range(plan.total):
                grad_t[me[DOWN] ^ places[u], :, k * rows : (k + 1) * rows] = turned[u * unit : (u + 1) * unit]

    for k in range(split):
        up[:, k * sub : (k + 1) * sub] = ups[k][...]
        down[k * sub : (k + 1) * sub, :] = downs[k][...]
    bias = jnp.concatenate([b[...] for b in biases], 1)
    bias_grad = jnp.zeros((1, tile), F32)
    for k, (g_ref, out, e) in enumerate(((g0_ref, out_ref, e_ref), (g1_ref, out_acc, e_acc))):
        span = slice(k * rows, (k + 1) * rows)
        pre = dot(normed_ref[span, :], up[...]) + bias
        cdf = 0.5 * (1.0 + lax.erf(pre * np.float32(0.5**0.5)))
        active = (pre * cdf).astype(BF)
        active_all[span, :] = active
        slope = cdf + pre * jnp.exp(pre * pre * -0.5) * np.float32(0.3989422804014327)
        out[...] += dot(active, down[...])
        pre_grad = slope * dot(g_ref[...], down[...], NT)
        low = pre_grad.astype(BF)
        e[...] += dot(low, up[...], NT)
        low_t[:, span] = pre_grad.T.astype(BF)
        bias_grad = bias_grad + column_sum(low.astype(F32))
    bias_grad_ref[0] = bias_grad
    half = plan.total // 2
    turned = grad_t[...].reshape(d, 2 * rows)
    down_t = dot(turned, active_all[...]).astype(BF)
    down_kept[...] = down_t[: half * unit]
    down_sent[...] = down_t[half * unit :]
    up_t = dot(low_t[...], normed_ref[...]).astype(BF)
    block = tile // plan.subs

    def store(ref):
        for k in range(plan.subs):
            ref[me[SUB] ^ k] = up_t[k * block : (k + 1) * block]

    later = step >= pl.num_programs(0) // 2
    pl.when(later)(lambda: store(up_kept))
    pl.when(jnp.logical_not(later))(lambda: store(up_sent))

    @pl.when(step == pl.num_programs(0) - 1)
    def _():
        out_other_ref[...] = out_acc[...].astype(BF)
        e_other_ref[...] = e_acc[...].astype(BF)


def feed(me, plan, normed, g0, g1, w_up, bias_up, w_down):
    rows, d = g0.shape
    ff = plan.ff
    tiles, subs, block = plan.tiles, plan.subs, plan.block
    tile = subs * block
    half = tiles // 2
    outer, inner = plan.owners(plan.outer), plan.owners(plan.inner)
    if block % 128 == 0:
        split = subs
        stride = [o[0] * plan.heads for o in outer]

        def column(k):
            s, h = inner[k]

            def at(i, me):
                t = (tiles - 1 - i) ^ me[TILE]
                value = stride[0]
                for q in range(1, tiles):
                    value = jnp.where(t == q, stride[q], value)
                return value + s * plan.heads + h + me[CORE]

            return at

        columns = [column(k) for k in range(subs)]
    else:
        split = 1
        order = np.asarray(
            [[(o[0] + s) * plan.heads + h for s, h in inner] for o in outer], np.int32
        ).reshape(-1)
        order = jnp.asarray(order) + me[CORE]
        w_up = jnp.take(w_up.reshape(d, plan.total, block), order, axis=1).reshape(d, ff // 2)
        w_down = jnp.take(w_down.reshape(plan.total, block, d), order, axis=0).reshape(ff // 2, d)
        bias_up = jnp.take(bias_up.reshape(1, plan.total, block), order, axis=1).reshape(1, ff // 2)
        columns = [lambda i, me: (tiles - 1 - i) ^ me[TILE]]
    sub = tile // split
    one = pl.Buffered(1)
    whole = pl.BlockSpec((rows, d), lambda i, me: (0, 0))
    whole_in = pl.BlockSpec((rows, d), lambda i, me: (0, 0), pipeline_mode=one)

    def up_at(first):
        return lambda i, me: (jnp.clip(half - 1 - (i - first), 0, half - 1), 0, 0)

    down_block = pl.BlockSpec((d // 2, tile), lambda i, me: (0, (tiles - 1 - i) ^ me[TILE]))
    return pl.pallas_call(
        functools.partial(feed_kernel, plan, split),
        grid_spec=pltpu.PrefetchScalarGridSpec(
            num_scalar_prefetch=1,
            grid=(tiles,),
            in_specs=[pl.BlockSpec((2 * rows, d), lambda i, me: (0, 0), pipeline_mode=one), whole_in, whole_in]
            + [pl.BlockSpec((d, sub), lambda i, me, c=c: (0, c(i, me))) for c in columns]
            + [pl.BlockSpec((1, sub), lambda i, me, c=c: (0, c(i, me))) for c in columns]
            + [pl.BlockSpec((sub, d), lambda i, me, c=c: (c(i, me), 0)) for c in columns],
            out_specs=[
                whole, whole, whole, whole,
                pl.BlockSpec((subs, block, d), up_at(half)),
                pl.BlockSpec((subs, block, d), up_at(0)),
                down_block,
                down_block,
                pl.BlockSpec((1, 1, tile), lambda i, me: ((tiles - 1 - i) ^ me[TILE], 0, 0)),
            ],
            scratch_shapes=[
                pltpu.VMEM((rows, d), F32),
                pltpu.VMEM((rows, d), F32),
                pltpu.VMEM((plan.total, d // plan.total, 2 * rows), BF),
                pltpu.VMEM((d, tile), BF),
                pltpu.VMEM((tile, d), BF),
                pltpu.VMEM((2 * rows, tile), BF),
                pltpu.VMEM((tile, 2 * rows), BF),
            ],
        ),
        out_shape=[
            shape((rows, d), F32),
            shape((rows, d), BF),
            shape((rows, d), F32),
            shape((rows, d), BF),
            shape((half * subs, block, d), BF),
            shape((half * subs, block, d), BF),
            shape((d // 2, ff // 2), BF),
            shape((d // 2, ff // 2), BF),
            shape((tiles, 1, tile), F32),
        ],
        compiler_params=params(),
        name="feed",
    )(me, normed, g0, g1, *[w_up] * split, *[bias_up] * split, *[w_down] * split)


def order_kernel(me, in_ref, out_ref):
    out_ref[...] = in_ref[...]


def order_columns(me, w_qkv, heads):
    d, columns = w_qkv.shape
    pairs = d // heads // PAIR
    parts = d // PAIR

    def source(i, me):
        p, rest = i // (3 * heads), i % (3 * heads)
        return 0, (rest % 3) * parts + (me[HEAD] ^ (rest // 3)) * pairs + p

    return pl.pallas_call(
        order_kernel,
        grid_spec=pltpu.PrefetchScalarGridSpec(
            num_scalar_prefetch=1,
            grid=(columns // PAIR,),
            in_specs=[pl.BlockSpec((d, PAIR), source)],
            out_specs=pl.BlockSpec((d, PAIR), lambda i, me: (0, i)),
        ),
        out_shape=shape((d, columns), BF),
        name="order_columns",
    )(me, w_qkv)


def product_kernel(heads, p, units, me, *refs):
    grads, normed = refs[:heads], refs[heads : 2 * heads]
    out_ref, sums_ref = refs[-2:]
    total = sums = None
    for g_ref, n_ref in zip(grads, normed):
        grad = g_ref[...].astype(F32)
        part, column = dot(grad.T.astype(BF), n_ref[...]), column_sum(grad)
        total = part if total is None else total + part
        sums = column if sums is None else sums + column
    sums_ref[...] = sums
    low = total.astype(BF)
    unit = low.shape[0] // units
    for u in range(units):
        out_ref[me[QKV + p * units + u]] = low[u * unit : (u + 1) * unit]


def product(me, plan, p, grads, normed, before):
    heads = len(grads)
    rows, d = normed[0].shape
    unit, per_slot, _, _ = unit_plan(d, plan.scenes, plan.heads)
    dims = (per_slot * plan.scenes, unit, d)
    extra = [] if before is None else [before]
    whole = pl.BlockSpec(dims, lambda i, me: (0, 0, 0))
    return pl.pallas_call(
        functools.partial(product_kernel if not extra else product_more, heads, p, 3 * PAIR // unit),
        grid_spec=pltpu.PrefetchScalarGridSpec(
            num_scalar_prefetch=1,
            grid=(1,),
            in_specs=[pl.BlockSpec((rows, 3 * PAIR), lambda i, me: (0, 0))] * heads
            + [pl.BlockSpec((rows, d), lambda i, me: (0, 0))] * heads
            + [whole] * len(extra),
            out_specs=[whole, pl.BlockSpec((1, 3 * PAIR), lambda i, me: (0, 0))],
        ),
        out_shape=[shape(dims, BF), shape((1, 3 * PAIR), F32)],
        compiler_params=params(),
        name="product",
    )(me, *grads, *normed, *extra)


def product_more(heads, p, units, me, *refs):
    refs[-2][...] = refs[2 * heads][...]
    product_kernel(heads, p, units, me, *refs[: 2 * heads], *refs[-2:])


def e_kernel(heads, first, last, *refs):
    pieces, w_ref = refs[:heads], refs[heads]
    at = heads + 1
    total = None
    if not first:
        total = refs[at][...]
        at += 1
    for r, piece in enumerate(pieces):
        part = dot(piece[...], w_ref[:, r * 3 * PAIR : (r + 1) * 3 * PAIR], NT)
        total = part if total is None else total + part
    if not last:
        refs[at][...] = total
        return
    x_ref, gain_ref, grad_middle_ref, out_ref, sums_ref = refs[at:]
    hat, scale = norm_parts(x_ref[...].astype(F32))
    out_ref[...] = (grad_middle_ref[...] + norm_back(hat, scale, gain_ref[...], total)).astype(BF)

    @pl.when(pl.program_id(0) == 0)
    def _():
        sums_ref[...] = jnp.zeros_like(sums_ref)

    sums_ref[0:1] += column_sum(total * hat)
    sums_ref[1:2] += column_sum(total)


def e_one(p, pieces, w_rel, before, finish):
    heads = len(pieces)
    rows = pieces[0].shape[0]
    d = w_rel.shape[0]
    tile = 128
    block = pl.BlockSpec((tile, d), lambda i: (i, 0))
    in_specs = [pl.BlockSpec((tile, 3 * PAIR), lambda i: (i, 0))] * heads
    in_specs += [pl.BlockSpec((d, heads * 3 * PAIR), lambda i: (0, p))]
    args = [*pieces, w_rel]
    if before is not None:
        in_specs.append(block)
        args.append(before)
    if finish is None:
        out_specs, out_shape = block, shape((rows, d), F32)
    else:
        in_specs += [block, pl.BlockSpec((1, d), lambda i: (0, 0)), block]
        args += list(finish)
        out_specs = [block, pl.BlockSpec((2, d), lambda i: (0, 0))]
        out_shape = [shape((rows, d), BF), shape((2, d), F32)]
    return pl.pallas_call(
        functools.partial(e_kernel, heads, before is None, finish is not None),
        grid=(rows // tile,),
        in_specs=in_specs,
        out_specs=out_specs,
        out_shape=out_shape,
        compiler_params=params(),
        name="e_one",
    )(*args)


def swap(value, axis, bit):
    size = lax.axis_size(axis)
    return lax.ppermute(value, axis, [(i, i ^ bit) for i in range(size)])


def added(a, b):
    return (a.astype(F32) + b.astype(F32)).astype(a.dtype)


def reduce_stages(kept, sent, stages):
    for k, (axis, bit) in enumerate(stages):
        got = swap(sent, axis, bit)
        if k + 1 == len(stages):
            return added(kept, got)
        half = kept.shape[0] // 2
        sent = added(kept[half:], got[half:])
        kept = added(kept[:half], got[:half])


def halve(blocks, axis, position, bit):
    mine = (lax.axis_index(axis) // bit) % 2
    kept = lax.dynamic_index_in_dim(blocks, mine, position, keepdims=False)
    sent = lax.dynamic_index_in_dim(blocks, 1 - mine, position, keepdims=False)
    return kept + swap(sent, axis, bit)


def scatter_axis(blocks, axis, position):
    size = blocks.shape[position]
    bit = 1
    while bit < size:
        dims = blocks.shape
        split = dims[:position] + (dims[position] // 2, 2) + dims[position + 1 :]
        blocks = halve(blocks.reshape(split), axis, position + 1, bit)
        bit *= 2
    return blocks.reshape(blocks.shape[:position] + blocks.shape[position + 1 :])


def scatter_vectors(vectors, scenes, heads):
    total = scenes * heads
    packed = jnp.concatenate([v.reshape(total, -1) for v in vectors], 1)
    blocks = packed.reshape(scenes, heads, -1)
    done = scatter_axis(scatter_axis(blocks, "head", 1), "scene", 0).reshape(-1)
    parts, at = [], 0
    for v in vectors:
        size = v.size // total
        parts.append(done[at : at + size])
        at += size
    return parts


def own_rows(summed, plan):
    unit, per_slot, _, rounds = unit_plan(plan.d, plan.scenes, plan.heads)
    me = lax.axis_index("scene") * plan.heads + lax.axis_index("head")
    result = jnp.zeros(summed.shape, summed.dtype)
    for chosen in rounds:
        source = np.zeros(plan.total, np.int32)
        target = np.zeros(plan.total, np.int32)
        for a, b, k, place in chosen:
            source[a] = k
            target[b] = place
        sent = lax.dynamic_index_in_dim(summed, jnp.asarray(source)[me], 0, keepdims=True)
        got = lax.ppermute(sent, ("scene", "head"), [(a, b) for a, b, _, _ in chosen])
        result = lax.dynamic_update_slice_in_dim(result, got, jnp.asarray(target)[me], 0)
    return result.reshape(per_slot * unit, -1)


def on_device(
    layer_in, scene_len, scene_group, scene_off, w_qkv, bias_q, bias_v, w_out, bias_out,
    w_up, bias_up, w_down, bias_down, gain_one, shift_one, gain_two, shift_two, grad_out,
):
    rows, d = layer_in.shape
    ff = w_up.shape[1]
    heads = lax.axis_size("head")
    scenes = lax.axis_size("scene")
    plan = Plan(d, ff, scenes, heads)
    total = plan.total
    width = d // heads
    pairs = width // PAIR
    capacity = rows * heads
    chips = heads // 2
    device = lax.axis_index("scene") * heads + lax.axis_index("head")
    me = lax.dynamic_index_in_dim(jnp.asarray(number_table(plan)), device, 0, keepdims=False)
    g_one, s_one, g_two, s_two, b_out, b_up = (
        v.astype(F32)[None] for v in (gain_one, shift_one, gain_two, shift_two, bias_out, bias_up)
    )

    normed = (norm_parts(layer_in.astype(F32))[0] * g_one + s_one).astype(BF)
    chunks = [normed]
    for r in range(1, heads):
        low = r & -r
        chunks.append(swap(chunks[r ^ low], "head", low))
    other_in = swap(layer_in, "head", 1)
    other_grad = swap(grad_out, "head", 1)

    zeros = jnp.zeros((d,), F32)
    bias_qkv = jnp.stack([bias_q.astype(F32), zeros, bias_v.astype(F32)])[:, None]
    marks_q, marks_k = marks(me, scene_len, scene_group, scene_off, rows, heads)
    w_rel = order_columns(me, w_qkv, heads)
    qkv = None
    for j in range(chips):
        qkv = project(me, j, chunks[2 * j], chunks[2 * j + 1], w_qkv, bias_qkv, capacity, width, qkv)

    outs, feats = [None] * chips, [None] * chips
    pieces = [None] * heads
    for j in list(range(1, chips)) + [0]:
        outs[j], feats[j] = attend(j, qkv, marks_q, marks_k, 2 * rows)
        pieces[2 * j] = outs[j] if j == 0 else swap(outs[j], "head", 2 * j)
    for j in range(chips):
        pieces[2 * j + 1] = swap(pieces[2 * j], "head", 1)

    middle, normed_two = merge(me, pieces, w_out, layer_in, other_in, b_out, g_two, s_two)
    out_own, out_other, e_own, e_other, up_kept, up_sent, down_kept, down_sent, up_bias = feed(
        me, plan, normed_two, grad_out, other_grad, w_up, b_up, w_down
    )
    e_more = swap(e_other, "head", 1)
    out_more = swap(out_other, "head", 1)
    grad_middle, branch, *back = middle_back(
        me, e_own, e_more, middle, grad_out, g_two, w_out, heads
    )
    early = back.pop()
    head_grads = [p if r == 0 else swap(p, "head", r) for r, p in enumerate(back)]

    up = reduce_stages(up_kept, up_sent, plan.up_stages)
    down = reduce_stages(down_kept, down_sent, plan.down_stages)
    out_units = out_grad(me, plan, branch, pieces)
    half = total // 2
    out = reduce_stages(out_units[:half], out_units[half:], plan.out_stages)

    owner = [list(o) for o in plan.owners(plan.up_stages)]
    sorted_to = np.zeros(total // 2, np.int32)
    for k, (s, h) in enumerate(owner):
        sorted_to[s * chips + h // 2] = k
    up_parts = jnp.take(up_bias.reshape(total // 2, plan.block), jnp.asarray(sorted_to), axis=0)
    up_parts = up_parts.reshape(scenes, chips, 1, plan.block)
    cores = jnp.arange(2, dtype=jnp.int32)[None, None, :, None]
    up_full = jnp.where(cores == me[CORE], up_parts, 0.0)
    early_parts = scatter_vectors([early[0], early[1], early[2], early[3], up_full], scenes, heads)

    token_grads, e, units, sums = [], None, None, []
    states = [None] * pairs
    for j in range(chips):
        for p in range(pairs):
            carried, olds = (None, []) if j == 0 else states[p]
            result = attend_back(
                j, p, heads, qkv, feats[j], marks_k, outs[j], head_grads[2 * j], head_grads[2 * j + 1],
                carried, olds,
            )
            if j + 1 < chips:
                states[p] = (result[1:], olds + [result[0]])
                continue
            moved = [g if r == 0 else swap(g, "head", r) for r, g in enumerate(result)]
            token_grads.append(moved)
            units, column = product(me, plan, p, result, chunks, units)
            sums.append(column)
    for p in range(pairs):
        finish = (layer_in, g_one, grad_middle) if p + 1 == pairs else None
        e = e_one(p, token_grads[p], w_rel, e, finish)
    grad_in, late = e

    slots = units.reshape((scenes, -1) + units.shape[1:])
    summed = reduce_stages(slots[: scenes // 2], slots[scenes // 2 :], plan.qkv_stages)
    grad_w_qkv = own_rows(summed.reshape((-1,) + units.shape[1:]), plan)

    mine = jnp.concatenate(sums, 0).reshape(pairs, 3, PAIR)
    devices = jnp.arange(heads, dtype=jnp.int32)[:, None]
    bias_parts = [
        jnp.where(devices == me[HEAD], mine[:, k].reshape(1, width), 0.0) for k in (0, 2)
    ]
    late_parts = scatter_vectors([late[0], late[1], *bias_parts], scenes, heads)

    layer_out = (
        middle + out_own + out_more.astype(F32) + bias_down.astype(F32)[None]
    ).astype(BF)

    unit = d // total
    rest = swap(down[unit:], "head", 1)
    both = jnp.stack([down[:unit], rest])
    both = jnp.where(me[CORE] == 0, both, both[::-1])
    both = both.reshape(2, unit, total // 2, plan.block)
    both = jnp.take(both, jnp.asarray(sorted_to), axis=2).reshape(2, unit, scenes, chips, plan.block)
    grad_w_down = both.astype(F32).transpose(2, 3, 0, 4, 1).reshape(ff, unit)
    grad_w_out = out.reshape(heads, unit, width).astype(F32).transpose(0, 2, 1).reshape(d, unit)
    return (
        layer_out,
        grad_in,
        grad_w_qkv.astype(F32).T,
        late_parts[2],
        late_parts[3],
        grad_w_out,
        early_parts[0],
        up.reshape(plan.block, d).astype(F32).T,
        early_parts[4],
        grad_w_down,
        early_parts[1],
        late_parts[0],
        late_parts[1],
        early_parts[2],
        early_parts[3],
    )


def solution(mesh):
    rows, whole, part = P(("scene", "head"), None), P(), P(("scene", "head"))
    columns = P(None, ("scene", "head"))

    return jax.shard_map(
        on_device,
        mesh=mesh,
        in_specs=(rows,) + (whole,) * 16 + (rows,),
        out_specs=(
            rows, rows, columns, part, part, columns, part, columns, part, columns,
            part, part, part, part, part,
        ),
        check_vma=False,
    )
```
